32 devices in a mesh: groups: 2 (over x), views: 16 (over z, y, core).
Axes of the slice: x: 2, y: 2, z: 4, core: 2. Of those that a mesh axis runs over, the one named last changes fastest.
Arguments:
- tokens: bfloat16 [32, 128, 1024], P(('groups', 'views')), parts along dimension 0, may hold values from -6 to 6
- in_gain: float32 [1024], replicated, may hold values from 0.7 to 6, as said below
- w_query: bfloat16 [1024, 1024], replicated, may hold values from -0.1875 to 0.1875
- w_key: bfloat16 [1024, 1024], replicated, may hold values from -0.1875 to 0.1875
- w_value: bfloat16 [1024, 1024], replicated, may hold values from -0.1875 to 0.1875
- w_out: bfloat16 [1024, 1024], replicated, may hold values from -0.1875 to 0.1875
- out_gain: float32 [1024], replicated, may hold values from 0.1 to 1.9
- covis_list: int32 [32, 12], P(('groups', 'views')), parts along dimension 0, may hold values from 0 to 15, as said below
- covis_count: int32 [32], P(('groups', 'views')), parts along dimension 0, may hold values from 2 to 12
Outputs:
- mixed: bfloat16 [32, 128, 1024], P(('groups', 'views')), parts along dimension 0
The draws below stay inside these ranges and needn't reach their ends.
There are 2 independent parts, one for each index of `groups`. The reference program is written for one: setup_inputs(seed, part) draws one part's arguments, and reference() takes and returns one part's arrays. A program takes and returns all parts, laid end to end along the dimension named above; an argument that names none is the same for every part. Nothing has to cross between parts.
Inputs may be any that keep to these rules, and one draw needn't show every extreme that they name: `covis_list`: row v lists 12 distinct view ids w, each with w - v modulo 16 among -6 to -1 and 1 to 6; only the first covis_count[v] entries are covisible views, the others are not used. `in_gain`: positive gains.
All inputs are finite; a program needn't handle non-finite values.
Results may differ from the reference program's by a relative error of at most 0.0085.
The reference program's roundings to bfloat16 on the way (of `normed`, `weights` and `head_normed`) count: a program that leaves them out, or rounds other values in their place, can miss the bound.
Values may be sent and summed in bfloat16 or wider, within the bound.
A program may use at most 128 MiB of HBM per device.

```python
import jax
import jax.numpy as jnp
from jax import lax

D = 1024
HEADS = 16
HEAD_DIM = 64
TOK_VIEW = 128
REACH = 6
MAXCOV = 12
VIEWS = 16


def draw_in_gain(key, part):
    return jax.random.uniform(key, (D,), jnp.float32, 0.7, 1.3)


def covis_tables(key):
    base = jax.random.fold_in(key, 11)
    key_first, key_second, key_pick, key_other, key_order = jax.random.split(base, 5)
    span = 2 * REACH
    first = jax.random.randint(key_first, (VIEWS,), 0, span - 1)
    second = jax.random.randint(key_second, (VIEWS,), 0, span - 1)
    counts = 2 + first * second // (span - 2)
    pick = jax.random.randint(key_pick, (), 0, VIEWS)
    other = (pick + 1 + jax.random.randint(key_other, (), 0, VIEWS - 1)) % VIEWS
    counts = counts.at[pick].set(span).at[other].set(2)
    slot = jnp.arange(span, dtype=jnp.int32)
    offsets = jnp.where(slot < REACH, slot - REACH, slot - REACH + 1)
    ranking = jax.random.randint(key_order, (VIEWS, span), 0, 1 << 20) * span + slot[None, :]
    order = jnp.argsort(ranking, axis=1)
    chosen = offsets[order]
    ids = (jnp.arange(VIEWS, dtype=jnp.int32)[:, None] + chosen) % VIEWS
    return (ids.astype(jnp.int32), counts.astype(jnp.int32))


def draw_covis_list(key, part):
    return covis_tables(key)[0]


def draw_covis_count(key, part):
    return covis_tables(key)[1]


def level_of(rng, shape, shards, smallest, top_value):
    def one(position, parts):
        steps = jax.random.uniform(jax.random.fold_in(jax.random.fold_in(rng, 6), position), (parts,), jnp.float32, smallest / len(shards), top_value / len(shards))
        return jnp.repeat(jnp.exp(steps), shape[position] // parts).reshape((-1,) + (1,) * (len(shape) - position - 1))

    factor_of = one(*shards[0])
    for cut in shards[1:]:
        factor_of = factor_of * one(*cut)
    return factor_of


def gaussian(stream_key, extent, width, limit, cuts=(), held_as=jnp.bfloat16):
    loudness = level_of(stream_key, extent, cuts, -0.22, 0.18) if cuts else 1.0
    values = jax.random.normal(stream_key, extent, jnp.float32) * width * loudness
    return jnp.minimum(jnp.maximum(values, -limit), limit).astype(held_as)


def setup_inputs(seed: int = 0, part: int = 0) -> dict:
    arg_keys = jax.random.split(jax.random.key(seed), 10)
    part_keys = jax.random.split(jax.random.fold_in(arg_keys[9], part), 10)
    return {
        "tokens": gaussian(part_keys[0], (VIEWS, TOK_VIEW, D), 1.0, 6.0, ((0, 16),)),
        "in_gain": draw_in_gain(jax.random.fold_in(arg_keys[9], 71), part),
        "w_query": gaussian(arg_keys[2], (D, D), D ** -0.5, 0.1875),
        "w_key": gaussian(arg_keys[3], (D, D), D ** -0.5, 0.1875),
        "w_value": gaussian(arg_keys[4], (D, D), D ** -0.5, 0.1875),
        "w_out": gaussian(arg_keys[5], (D, D), D ** -0.5, 0.1875),
        "out_gain": jnp.clip(1.0 + 0.18 * jax.random.normal(arg_keys[6], (D,), jnp.float32), 0.1, 1.9),
        "covis_list": draw_covis_list(jax.random.fold_in(jax.random.fold_in(arg_keys[9], part), 71), part),
        "covis_count": draw_covis_count(jax.random.fold_in(jax.random.fold_in(arg_keys[9], part), 71), part),
    }


def rms_scale(values, gain):
    mean_sq = lax.optimization_barrier(jnp.mean(values * values, axis=-1, keepdims=True))
    return values * lax.rsqrt(mean_sq + 1e-06) * gain

def reference(tokens, in_gain, w_query, w_key, w_value, w_out, out_gain, covis_list, covis_count):
    normed = rms_scale(tokens.astype(jnp.float32), in_gain).astype(jnp.bfloat16)
    flat = normed.reshape(VIEWS * TOK_VIEW, D)
    query = jnp.dot(flat, w_query, preferred_element_type=jnp.float32).astype(jnp.bfloat16).reshape(VIEWS, TOK_VIEW, HEADS, HEAD_DIM)
    keys = jnp.dot(flat, w_key, preferred_element_type=jnp.float32).astype(jnp.bfloat16).reshape(VIEWS, TOK_VIEW, HEADS, HEAD_DIM)
    values = jnp.dot(flat, w_value, preferred_element_type=jnp.float32).astype(jnp.bfloat16).reshape(VIEWS, TOK_VIEW, HEADS, HEAD_DIM)
    offsets = jnp.arange(-REACH, REACH + 1, dtype=jnp.int32)
    slots = jnp.arange(MAXCOV, dtype=jnp.int32)
    scale = HEAD_DIM ** (-0.5)
    gain_heads = out_gain.reshape(HEADS, HEAD_DIM)

    def one_view(view):
        others = ((view + offsets) % VIEWS).astype(jnp.int32)
        valid = slots < covis_count[view]
        listed = jnp.any((covis_list[view][None, :] == others[:, None]) & valid[None, :], axis=1) | (offsets == 0)
        key_set = keys[others].reshape(-1, HEADS, HEAD_DIM).astype(jnp.float32)
        value_set = values[others].reshape(-1, HEADS, HEAD_DIM).astype(jnp.float32)
        scores = jnp.einsum('qhd,khd->qhk', query[view].astype(jnp.float32), key_set) * scale
        live = jnp.repeat(listed, TOK_VIEW)
        scores = jnp.where(live[None, None, :], scores, -jnp.inf)
        peak = lax.optimization_barrier(jnp.max(scores, axis=-1, keepdims=True))
        weights = jnp.exp(scores - peak)
        total = lax.optimization_barrier(jnp.sum(weights, axis=-1))
        numer = jnp.einsum('qhk,khd->qhd', weights.astype(jnp.bfloat16).astype(jnp.float32), value_set)
        attended = numer / total[..., None]
        head_normed = rms_scale(attended, gain_heads).astype(jnp.bfloat16).reshape(TOK_VIEW, D)
        update = jnp.dot(head_normed, w_out, preferred_element_type=jnp.float32)
        return (tokens[view].astype(jnp.float32) + update).astype(jnp.bfloat16)
    return lax.map(one_view, jnp.arange(VIEWS, dtype=jnp.int32))
```

```python
import functools

import jax
import jax.numpy as jnp
from jax import lax
from jax.experimental import pallas as pl
from jax.experimental.pallas import tpu as pltpu
from jax.sharding import PartitionSpec as P

HEADS = 16
HEAD_DIM = 64
REACH = 6
SPAN = REACH // 2
SLOTS = 2 * SPAN + 1
MESH = pl.DeviceIdType.MESH
INF = float("inf")

GRID_ROUTE = {1: (0, "down"), 2: (0, "up"), 3: (0, "side"), 4: (1, "side"), 5: (3, "up"), 6: (4, "down")}
GRID_EVENTS = {0: (1, 3, 2), 2: (5, 4), 4: (6,)}


def ring_route():
    route = {1: (0, "down"), 2: (0, "up")}
    for slot in range(3, SLOTS):
        route[slot] = (slot - 2, "down" if slot % 2 else "up")
    events = {2 * i: (2 * i + 1, 2 * i + 2) for i in range(SPAN)}
    return route, events


def is_grid(chips):
    return SPAN == 3 and chips == 2 * SPAN + 2


def neighbour(chip, sign, way, chips):
    if is_grid(chips):
        row, col = chip // 2, chip % 2
        rows = chips // 2
        if way == "side":
            return row * 2 + 1 - col
        step = sign if way == "up" else -sign
        return (row + step + rows) % rows * 2 + col
    step = sign if way == "up" else -sign
    return (chip + step + chips) % chips


def slot_chip(chip, sign, slot, chips):
    if is_grid(chips):
        row, col = chip // 2, chip % 2
        rows = chips // 2
        step, flip = {0: (0, 0), 1: (1, 0), 2: (-1, 0), 3: (0, 1), 4: (1, 1), 5: (-1, 1), 6: (2, 1)}[slot]
        new_col = 1 - col if flip else col
        return (row + step * sign + 2 * rows) % rows * 2 + new_col
    dist = (slot + 1) // 2
    step = dist if slot % 2 else -dist
    return (chip + step * sign + 2 * chips) % chips


def body(
    views, tok_hbm, in_gain, wq_hbm, wk_hbm, wv_hbm, wo_hbm, out_gain, flags,
    out_ref,
    buf, wq, wk, wv, wo, qpad, kbuf, vtbuf, peak, total, acc, peer_flags, mask, hn, hn_in,
    load_sem, send_sem, recv_sem, pass_send, pass_recv, misc_send, misc_recv,
):
    chips = views // 2
    me = lax.axis_index("views")
    chip, core = me // 2, me % 2
    sign = 1 - 2 * core
    partner = chip * 2 + 1 - core
    half = wq.shape[1]
    rows = tok_hbm.shape[0]
    heads = half // HEAD_DIM
    if is_grid(chips):
        route, events = GRID_ROUTE, GRID_EVENTS
        ways = ("up", "down", "side")
    else:
        route, events = ring_route()
        ways = ("up", "down")

    def device(way):
        return {"views": neighbour(chip, sign, way, chips) * 2 + core}

    columns = pl.ds(pl.multiple_of(core * half, half), half)
    loads = [
        pltpu.make_async_copy(tok_hbm, buf.at[0, 0], load_sem.at[0]),
        pltpu.make_async_copy(wq_hbm.at[:, columns], wq, load_sem.at[1]),
        pltpu.make_async_copy(wk_hbm.at[:, columns], wk, load_sem.at[2]),
        pltpu.make_async_copy(wv_hbm.at[:, columns], wv, load_sem.at[3]),
        pltpu.make_async_copy(wo_hbm, wo, load_sem.at[4]),
    ]

    barrier = pltpu.get_barrier_semaphore()
    for way in ways:
        pl.semaphore_signal(barrier, inc=1, device_id=device(way), device_id_type=MESH)
    pl.semaphore_signal(barrier, inc=1, device_id={"views": partner}, device_id_type=MESH)
    for load in loads:
        load.start()
    pl.semaphore_wait(barrier, len(ways) + 1)

    def hop(slot):
        source, way = route[slot]
        return pltpu.make_async_remote_copy(
            src_ref=tok_hbm if source == 0 else buf.at[source, 0],
            dst_ref=buf.at[slot, 0],
            send_sem=send_sem.at[slot],
            recv_sem=recv_sem.at[slot],
            device_id=device(way),
            device_id_type=MESH,
        )

    def hand_over(slot):
        return pltpu.make_async_remote_copy(
            src_ref=tok_hbm if isinstance(slot, int) and slot == 0 else buf.at[slot, 0],
            dst_ref=buf.at[slot, 1],
            send_sem=pass_send.at[slot],
            recv_sem=pass_recv.at[slot],
            device_id={"views": partner},
            device_id_type=MESH,
        )

    flag_copy = pltpu.make_async_remote_copy(
        src_ref=flags, dst_ref=peer_flags, send_sem=misc_send.at[0], recv_sem=misc_recv.at[0],
        device_id={"views": partner}, device_id_type=MESH,
    )
    swap = pltpu.make_async_remote_copy(
        src_ref=hn.at[1], dst_ref=hn_in, send_sem=misc_send.at[1], recv_sem=misc_recv.at[1],
        device_id={"views": partner}, device_id_type=MESH,
    )
    hand_over(0).start()
    flag_copy.start()
    for slot in route:
        if route[slot][0] == 0:
            hop(slot).start()

    peak[...] = jnp.full(peak.shape, -INF, jnp.float32)
    total[...] = jnp.zeros(total.shape, jnp.float32)
    acc[...] = jnp.zeros(acc.shape, jnp.float32)
    flag_copy.wait_recv()
    for slot in range(SLOTS):
        for bank in range(2):
            own_row = flags[pl.ds(2 * slot + bank, 1), :]
            peer_row = peer_flags[pl.ds(2 * slot + 1 - bank, 1), :]
            mask[slot, pl.ds(bank, 1), :] = jnp.concatenate([own_row, peer_row], axis=1)

    def normed_of(slot):
        raw = buf[slot].reshape(2 * rows, buf.shape[-1]).astype(jnp.float32)
        mean_sq = jnp.mean(raw * raw, axis=-1, keepdims=True)
        return (raw * lax.rsqrt(mean_sq + 1e-6) * in_gain[...]).astype(jnp.bfloat16)

    loads[0].wait()
    hand_over(0).wait_recv()
    loads[1].wait()
    query = jnp.dot(normed_of(0), wq[...], preferred_element_type=jnp.float32).astype(jnp.bfloat16)
    query = query.astype(jnp.float32) * HEAD_DIM ** (-0.5)
    query_t = query.T.astype(jnp.bfloat16)
    zero = jnp.zeros((HEAD_DIM, 2 * rows), jnp.bfloat16)
    for h in range(heads):
        mine = query_t[h * HEAD_DIM:(h + 1) * HEAD_DIM, :]
        qpad[h] = jnp.concatenate([mine, zero] if h % 2 == 0 else [zero, mine], axis=0)
    loads[2].wait()
    loads[3].wait()

    def chunk(slot, carry):
        @pl.when(slot > 0)
        def _():
            hand_over(slot).wait_recv()

        normed = normed_of(slot)
        kbuf[...] = jnp.dot(normed, wk[...], preferred_element_type=jnp.float32).astype(jnp.bfloat16)
        value = jnp.dot(normed, wv[...], preferred_element_type=jnp.float32)
        vtbuf[...] = value.T.astype(jnp.bfloat16)
        live = mask[slot]
        on_first = live[0:1, :] > 0.5
        on_second = live[1:2, :] > 0.5
        for h in range(heads):
            pair = (h // 2) * 2 * HEAD_DIM
            feats = slice(h * HEAD_DIM, (h + 1) * HEAD_DIM)
            scores = jnp.dot(
                kbuf[:, pair:pair + 2 * HEAD_DIM], qpad[h], preferred_element_type=jnp.float32
            )
            first, second = scores[:rows], scores[rows:]
            old = peak[h:h + 1, :]
            new = jnp.maximum(
                jnp.where(on_first, jnp.max(first, axis=0, keepdims=True), -INF),
                jnp.where(on_second, jnp.max(second, axis=0, keepdims=True), -INF),
            )
            new = jnp.maximum(old, new)
            e_first = jnp.exp(first - jnp.where(on_first, new, INF))
            e_second = jnp.exp(second - jnp.where(on_second, new, INF))
            keep = jnp.exp(old - new)
            peak[h:h + 1, :] = new
            total[h:h + 1, :] = total[h:h + 1, :] * keep + jnp.sum(e_first + e_second, axis=0, keepdims=True)
            weights = jnp.concatenate([e_first, e_second], axis=0).astype(jnp.bfloat16)
            acc[feats, :] = acc[feats, :] * keep + jnp.dot(
                vtbuf[feats, :], weights, preferred_element_type=jnp.float32
            )

        for after, arrivals in events.items():
            @pl.when(slot == after)
            def _(arrivals=arrivals):
                for got in arrivals:
                    hop(got).wait_recv()
                    hand_over(got).start()
                    for later in route:
                        if route[later][0] == got:
                            hop(later).start()
        return carry

    lax.fori_loop(0, SLOTS, chunk, 0)

    gain = out_gain[:, columns]
    pieces = []
    for h in range(heads):
        attended = acc[h * HEAD_DIM:(h + 1) * HEAD_DIM, :] / total[h:h + 1, :]
        mean_sq = jnp.mean(attended * attended, axis=0, keepdims=True)
        pieces.append(attended * lax.rsqrt(mean_sq + 1e-6))
    head_normed = (jnp.concatenate(pieces, axis=0).T * gain).astype(jnp.bfloat16)
    hn[1] = head_normed[rows:]
    swap.start()
    hn[0] = head_normed[:rows]
    loads[4].wait()
    others = pl.ds(pl.multiple_of((1 - core) * half, half), half)
    update = jnp.dot(hn[0], wo[columns, :], preferred_element_type=jnp.float32)
    swap.wait_recv()
    update = update + jnp.dot(hn_in[...], wo[others, :], preferred_element_type=jnp.float32)
    out_ref[...] = (buf[0, 0].astype(jnp.float32) + update).astype(out_ref.dtype)

    for slot in route:
        hop(slot).wait_send()
    for slot in range(SLOTS):
        hand_over(slot).wait_send()
    flag_copy.wait_send()
    swap.wait_send()


def on_device(tokens, in_gain, w_query, w_key, w_value, w_out, out_gain, covis_list, covis_count):
    views = lax.axis_size("views")
    chips = views // 2
    me = lax.axis_index("views")
    chip, core = me // 2, me % 2
    sign = 1 - 2 * core
    rows, width = tokens.shape[1:]
    half = width // 2
    ids = []
    for slot in range(SLOTS):
        ids.append(slot_chip(chip, sign, slot, chips) * 2 + core)
        ids.append(slot_chip(chip, -sign, slot, chips) * 2 + 1 - core)
    ids += [-1] * (16 - len(ids))
    ids = jnp.stack([jnp.asarray(i, jnp.int32) for i in ids])
    valid = jnp.arange(covis_list.shape[1], dtype=jnp.int32) < covis_count[0]
    listed = jnp.any((covis_list[0][None, :] == ids[:, None]) & valid[None, :], axis=1) | (ids == me)
    flags = jnp.broadcast_to(listed.astype(jnp.float32)[:, None], (16, rows))
    hbm = pl.BlockSpec(memory_space=pl.ANY)
    vmem = pl.BlockSpec(memory_space=pltpu.VMEM)
    bf16, f32 = jnp.bfloat16, jnp.float32
    heads = half // HEAD_DIM
    dma = pltpu.SemaphoreType.DMA
    out = pl.pallas_call(
        functools.partial(body, views),
        out_shape=jax.ShapeDtypeStruct((rows, width), tokens.dtype),
        in_specs=[hbm, vmem, hbm, hbm, hbm, hbm, vmem, vmem],
        out_specs=vmem,
        scratch_shapes=[
            pltpu.VMEM((SLOTS, 2, rows, width), bf16),
            pltpu.VMEM((width, half), bf16),
            pltpu.VMEM((width, half), bf16),
            pltpu.VMEM((width, half), bf16),
            pltpu.VMEM((width, width), bf16),
            pltpu.VMEM((heads, 2 * HEAD_DIM, 2 * rows), bf16),
            pltpu.VMEM((2 * rows, half), bf16),
            pltpu.VMEM((half, 2 * rows), bf16),
            pltpu.VMEM((heads, 2 * rows), f32),
            pltpu.VMEM((heads, 2 * rows), f32),
            pltpu.VMEM((half, 2 * rows), f32),
            pltpu.VMEM((16, rows), f32),
            pltpu.VMEM((SLOTS, 2, 2 * rows), f32),
            pltpu.VMEM((2, rows, half), bf16),
            pltpu.VMEM((rows, half), bf16),
            dma((5,)),
            dma((SLOTS,)),
            dma((SLOTS,)),
            dma((SLOTS,)),
            dma((SLOTS,)),
            dma((2,)),
            dma((2,)),
        ],
        compiler_params=pltpu.CompilerParams(
            collective_id=0, has_side_effects=True, vmem_limit_bytes=48 * 1024 * 1024
        ),
    )(tokens[0], in_gain[None], w_query, w_key, w_value, w_out, out_gain[None], flags)
    return out[None]


def solution(mesh):
    in_specs = (
        P(("groups", "views"), None, None),
        P(), P(), P(), P(), P(), P(),
        P(("groups", "views"), None),
        P(("groups", "views")),
    )
    out_specs = P(("groups", "views"), None, None)
    return jax.shard_map(on_device, mesh=mesh, in_specs=in_specs, out_specs=out_specs, check_vma=False)
```

```python
import functools

import jax
import jax.numpy as jnp
from jax import lax
from jax.experimental import pallas as pl
from jax.experimental.pallas import tpu as pltpu
from jax.sharding import PartitionSpec as P

HEADS = 16
HEAD_DIM = 64
REACH = 6
SPAN = REACH // 2
SLOTS = 2 * SPAN + 1
MESH = pl.DeviceIdType.MESH
INF = float("inf")

GRID_ROUTE = {1: (0, "down"), 2: (0, "up"), 3: (0, "side"), 4: (1, "side"), 5: (3, "up"), 6: (4, "down")}
GRID_EVENTS = {0: (1, 3, 2), 2: (5, 4), 4: (6,)}


def ring_route():
    route = {1: (0, "down"), 2: (0, "up")}
    for slot in range(3, SLOTS):
        route[slot] = (slot - 2, "down" if slot % 2 else "up")
    events = {2 * i: (2 * i + 1, 2 * i + 2) for i in range(SPAN)}
    return route, events


def is_grid(chips):
    return SPAN == 3 and chips == 2 * SPAN + 2


def neighbour(chip, sign, way, chips):
    if is_grid(chips):
        row, col = chip // 2, chip % 2
        rows = chips // 2
        if way == "side":
            return row * 2 + 1 - col
        step = sign if way == "up" else -sign
        return (row + step + rows) % rows * 2 + col
    step = sign if way == "up" else -sign
    return (chip + step + chips) % chips


def slot_chip(chip, sign, slot, chips):
    if is_grid(chips):
        row, col = chip // 2, chip % 2
        rows = chips // 2
        step, flip = {0: (0, 0), 1: (1, 0), 2: (-1, 0), 3: (0, 1), 4: (1, 1), 5: (-1, 1), 6: (2, 1)}[slot]
        new_col = 1 - col if flip else col
        return (row + step * sign + 2 * rows) % rows * 2 + new_col
    dist = (slot + 1) // 2
    step = dist if slot % 2 else -dist
    return (chip + step * sign + 2 * chips) % chips


def body(
    views, tok_hbm, in_gain_hbm, wq_hbm, wk_hbm, wv_hbm, wo_hbm, out_gain_hbm, list_hbm, count_hbm,
    out_ref,
    buf, wq, wk, wv, wo, in_gain, out_gain, lists, counts, qpad, kbuf, vtbuf, peak, total, acc, mask, hn, hn_in,
    load_sem, send_sem, recv_sem, pass_send, pass_recv, misc_send, misc_recv,
):
    chips = views // 2
    me = lax.axis_index("views")
    chip, core = me // 2, me % 2
    sign = 1 - 2 * core
    partner = chip * 2 + 1 - core
    half = wq.shape[1]
    rows = tok_hbm.shape[0]
    heads = half // HEAD_DIM
    if is_grid(chips):
        route, events = GRID_ROUTE, GRID_EVENTS
        ways = ("up", "down", "side")
    else:
        route, events = ring_route()
        ways = ("up", "down")

    def device(way):
        return {"views": neighbour(chip, sign, way, chips) * 2 + core}

    columns = pl.ds(pl.multiple_of(core * half, half), half)
    loads = [
        pltpu.make_async_copy(tok_hbm, buf.at[0, 0], load_sem.at[0]),
        pltpu.make_async_copy(wq_hbm.at[:, columns], wq, load_sem.at[1]),
        pltpu.make_async_copy(wk_hbm.at[:, columns], wk, load_sem.at[2]),
        pltpu.make_async_copy(wv_hbm.at[:, columns], wv, load_sem.at[3]),
        pltpu.make_async_copy(wo_hbm, wo, load_sem.at[4]),
        pltpu.make_async_copy(in_gain_hbm, in_gain, load_sem.at[5]),
        pltpu.make_async_copy(out_gain_hbm, out_gain, load_sem.at[6]),
        pltpu.make_async_copy(list_hbm, lists.at[0], load_sem.at[7]),
        pltpu.make_async_copy(count_hbm, counts.at[0], load_sem.at[8]),
    ]

    barrier = pltpu.get_barrier_semaphore()
    for way in ways:
        pl.semaphore_signal(barrier, inc=1, device_id=device(way), device_id_type=MESH)
    pl.semaphore_signal(barrier, inc=1, device_id={"views": partner}, device_id_type=MESH)
    for load in loads:
        load.start()
    pl.semaphore_wait(barrier, len(ways) + 1)

    def hop(slot):
        source, way = route[slot]
        return pltpu.make_async_remote_copy(
            src_ref=tok_hbm if source == 0 else buf.at[source, 0],
            dst_ref=buf.at[slot, 0],
            send_sem=send_sem.at[slot],
            recv_sem=recv_sem.at[slot],
            device_id=device(way),
            device_id_type=MESH,
        )

    def hand_over(slot):
        return pltpu.make_async_remote_copy(
            src_ref=tok_hbm if isinstance(slot, int) and slot == 0 else buf.at[slot, 0],
            dst_ref=buf.at[slot, 1],
            send_sem=pass_send.at[slot],
            recv_sem=pass_recv.at[slot],
            device_id={"views": partner},
            device_id_type=MESH,
        )

    list_copy = pltpu.make_async_remote_copy(
        src_ref=list_hbm, dst_ref=lists.at[1], send_sem=misc_send.at[0], recv_sem=misc_recv.at[0],
        device_id={"views": partner}, device_id_type=MESH,
    )
    count_copy = pltpu.make_async_remote_copy(
        src_ref=count_hbm, dst_ref=counts.at[1], send_sem=misc_send.at[2], recv_sem=misc_recv.at[2],
        device_id={"views": partner}, device_id_type=MESH,
    )
    swap = pltpu.make_async_remote_copy(
        src_ref=hn.at[1], dst_ref=hn_in, send_sem=misc_send.at[1], recv_sem=misc_recv.at[1],
        device_id={"views": partner}, device_id_type=MESH,
    )
    hand_over(0).start()
    list_copy.start()
    count_copy.start()
    for slot in route:
        if route[slot][0] == 0:
            hop(slot).start()

    peak[...] = jnp.full(peak.shape, -INF, jnp.float32)
    total[...] = jnp.zeros(total.shape, jnp.float32)
    acc[...] = jnp.zeros(acc.shape, jnp.float32)
    for load in loads[5:]:
        load.wait()
    list_copy.wait_recv()
    count_copy.wait_recv()
    ids = jnp.zeros((16, 1), jnp.int32)
    place = lax.broadcasted_iota(jnp.int32, (16, 1), 0)
    for slot in range(SLOTS):
        mine = slot_chip(chip, sign, slot, chips) * 2 + core
        other = slot_chip(chip, -sign, slot, chips) * 2 + 1 - core
        ids = jnp.where(place == 2 * slot, mine, jnp.where(place == 2 * slot + 1, other, ids))
    for side, query_view in enumerate((me, partner)):
        listed = lists[side]
        valid = lax.broadcasted_iota(jnp.int32, (16, listed.shape[1]), 1) < counts[side:side + 1, :]
        hits = jnp.where(((listed == ids) | (ids == query_view)) & valid, 1.0, 0.0)
        mask[:, side * rows:(side + 1) * rows] = jnp.broadcast_to(
            jnp.max(hits, axis=1, keepdims=True), (16, rows)
        )

    def normed_of(slot):
        raw = buf[slot].reshape(2 * rows, buf.shape[-1]).astype(jnp.float32)
        mean_sq = jnp.mean(raw * raw, axis=-1, keepdims=True)
        return (raw * lax.rsqrt(mean_sq + 1e-6) * in_gain[...]).astype(jnp.bfloat16)

    loads[0].wait()
    hand_over(0).wait_recv()
    loads[1].wait()
    query = jnp.dot(normed_of(0), wq[...], preferred_element_type=jnp.float32).astype(jnp.bfloat16)
    query = query.astype(jnp.float32) * HEAD_DIM ** (-0.5)
    query_t = query.T.astype(jnp.bfloat16)
    zero = jnp.zeros((HEAD_DIM, 2 * rows), jnp.bfloat16)
    for h in range(heads):
        mine = query_t[h * HEAD_DIM:(h + 1) * HEAD_DIM, :]
        qpad[h] = jnp.concatenate([mine, zero] if h % 2 == 0 else [zero, mine], axis=0)
    loads[2].wait()
    loads[3].wait()

    def chunk(slot, carry):
        @pl.when(slot > 0)
        def _():
            hand_over(slot).wait_recv()

        normed = normed_of(slot)
        kbuf[...] = jnp.dot(normed, wk[...], preferred_element_type=jnp.float32).astype(jnp.bfloat16)
        value = jnp.dot(normed, wv[...], preferred_element_type=jnp.float32)
        vtbuf[...] = value.T.astype(jnp.bfloat16)
        on_first = mask[pl.ds(2 * slot, 1), :] > 0.5
        on_second = mask[pl.ds(2 * slot + 1, 1), :] > 0.5
        for h in range(heads):
            pair = (h // 2) * 2 * HEAD_DIM
            feats = slice(h * HEAD_DIM, (h + 1) * HEAD_DIM)
            scores = jnp.dot(
                kbuf[:, pair:pair + 2 * HEAD_DIM], qpad[h], preferred_element_type=jnp.float32
            )
            first, second = scores[:rows], scores[rows:]
            old = peak[h:h + 1, :]
            new = jnp.maximum(
                jnp.where(on_first, jnp.max(first, axis=0, keepdims=True), -INF),
                jnp.where(on_second, jnp.max(second, axis=0, keepdims=True), -INF),
            )
            new = jnp.maximum(old, new)
            e_first = jnp.exp(first - jnp.where(on_first, new, INF))
            e_second = jnp.exp(second - jnp.where(on_second, new, INF))
            keep = jnp.exp(old - new)
            peak[h:h + 1, :] = new
            total[h:h + 1, :] = total[h:h + 1, :] * keep + jnp.sum(e_first + e_second, axis=0, keepdims=True)
            weights = jnp.concatenate([e_first, e_second], axis=0).astype(jnp.bfloat16)
            acc[feats, :] = acc[feats, :] * keep + jnp.dot(
                vtbuf[feats, :], weights, preferred_element_type=jnp.float32
            )

        for after, arrivals in events.items():
            @pl.when(slot == after)
            def _(arrivals=arrivals):
                for got in arrivals:
                    hop(got).wait_recv()
                    hand_over(got).start()
                    for later in route:
                        if route[later][0] == got:
                            hop(later).start()
        return carry

    lax.fori_loop(0, SLOTS, chunk, 0)

    gain = out_gain[:, columns]
    pieces = []
    for h in range(heads):
        attended = acc[h * HEAD_DIM:(h + 1) * HEAD_DIM, :] / total[h:h + 1, :]
        mean_sq = jnp.mean(attended * attended, axis=0, keepdims=True)
        pieces.append(attended * lax.rsqrt(mean_sq + 1e-6))
    head_normed = (jnp.concatenate(pieces, axis=0).T * gain).astype(jnp.bfloat16)
    hn[1] = head_normed[rows:]
    swap.start()
    hn[0] = head_normed[:rows]
    loads[4].wait()
    others = pl.ds(pl.multiple_of((1 - core) * half, half), half)
    update = jnp.dot(hn[0], wo[columns, :], preferred_element_type=jnp.float32)
    swap.wait_recv()
    update = update + jnp.dot(hn_in[...], wo[others, :], preferred_element_type=jnp.float32)
    out_ref[...] = (buf[0, 0].astype(jnp.float32) + update).astype(out_ref.dtype)

    for slot in route:
        hop(slot).wait_send()
    for slot in range(SLOTS):
        hand_over(slot).wait_send()
    list_copy.wait_send()
    count_copy.wait_send()
    swap.wait_send()


def on_device(tokens, in_gain, w_query, w_key, w_value, w_out, out_gain, covis_list, covis_count):
    views = lax.axis_size("views")
    rows, width = tokens.shape[1:]
    half = width // 2
    slots_listed = covis_list.shape[1]
    hbm = pl.BlockSpec(memory_space=pltpu.HBM)
    vmem = pl.BlockSpec(memory_space=pltpu.VMEM)
    bf16, f32 = jnp.bfloat16, jnp.float32
    heads = half // HEAD_DIM
    dma = pltpu.SemaphoreType.DMA
    out = pl.pallas_call(
        functools.partial(body, views),
        out_shape=jax.ShapeDtypeStruct((rows, width), tokens.dtype),
        in_specs=[hbm] * 9,
        out_specs=vmem,
        scratch_shapes=[
            pltpu.VMEM((SLOTS, 2, rows, width), bf16),
            pltpu.VMEM((width, half), bf16),
            pltpu.VMEM((width, half), bf16),
            pltpu.VMEM((width, half), bf16),
            pltpu.VMEM((width, width), bf16),
            pltpu.VMEM((1, width), f32),
            pltpu.VMEM((1, width), f32),
            pltpu.VMEM((2, 1, slots_listed), jnp.int32),
            pltpu.VMEM((2, 1), jnp.int32),
            pltpu.VMEM((heads, 2 * HEAD_DIM, 2 * rows), bf16),
            pltpu.VMEM((2 * rows, half), bf16),
            pltpu.VMEM((half, 2 * rows), bf16),
            pltpu.VMEM((heads, 2 * rows), f32),
            pltpu.VMEM((heads, 2 * rows), f32),
            pltpu.VMEM((half, 2 * rows), f32),
            pltpu.VMEM((16, 2 * rows), f32),
            pltpu.VMEM((2, rows, half), bf16),
            pltpu.VMEM((rows, half), bf16),
            dma((9,)),
            dma((SLOTS,)),
            dma((SLOTS,)),
            dma((SLOTS,)),
            dma((SLOTS,)),
            dma((3,)),
            dma((3,)),
        ],
        compiler_params=pltpu.CompilerParams(
            collective_id=0, has_side_effects=True, vmem_limit_bytes=60 * 1024 * 1024
        ),
    )(tokens[0], in_gain[None], w_query, w_key, w_value, w_out, out_gain[None], covis_list, covis_count)
    return out[None]


def solution(mesh):
    in_specs = (
        P(("groups", "views"), None, None),
        P(), P(), P(), P(), P(), P(),
        P(("groups", "views"), None),
        P(("groups", "views")),
    )
    out_specs = P(("groups", "views"), None, None)
    return jax.shard_map(on_device, mesh=mesh, in_specs=in_specs, out_specs=out_specs, check_vma=False)
```

```python
import functools

import jax
import jax.numpy as jnp
from jax import lax
from jax.experimental import pallas as pl
from jax.experimental.pallas import tpu as pltpu
from jax.sharding import PartitionSpec as P

HEADS = 16
HEAD_DIM = 64
REACH = 6
SPAN = REACH // 2
CHUNKS = 2 * SPAN + 1
PARTS = 4
MESH = pl.DeviceIdType.MESH
INF = float("inf")


def is_grid(chips):
    return chips == 2 * SPAN + 2


def ring_position(chip, chips):
    if not is_grid(chips):
        return chip
    row, col = chip // 2, chip % 2
    return row + col * (chips - 1 - 2 * row)


def ring_chip(position, chips):
    position = (position + chips) % chips
    if not is_grid(chips):
        return position
    col = position // (chips // 2)
    row = position + col * (chips - 1 - 2 * position)
    return 2 * row + col


def ring_route(chips):
    route = {1: (0, -1), 2: (0, 1)}
    last = CHUNKS + 1 if is_grid(chips) else CHUNKS
    for slot in range(3, last):
        route[slot] = (slot - 2, -1 if slot % 2 else 1)
    arrive, settle = {}, {}
    for first in range(1, last, 2):
        hops = (first + 1) // 2
        pair = [slot for slot in (first, first + 1) if slot in route]
        need = 2 * hops - 1
        if is_grid(chips) and hops >= SPAN:
            need = 2 * hops - 2
        for part in range(PARTS):
            after = need - 1
            if hops == 2 or not is_grid(chips) and hops == SPAN:
                after = need - 2 + part * 2 // PARTS
            if hops > SPAN:
                after = need - 2
            for slot in pair:
                arrive.setdefault(after, []).append((slot, part))
                settle.setdefault(need, []).append((slot, part))
    return route, arrive, settle


def slot_of(chunk, position, sign, chips):
    if not is_grid(chips):
        return chunk
    late = position % (chips // 2) // (chips // 4)
    ahead = (1 - 2 * late) * sign
    skipped = (SPAN + 1) - (ahead + 1) // 2
    return chunk + (chunk >= skipped).astype(jnp.int32)


def body(
    views, tok_hbm, in_gain_hbm, wq_hbm, wk_hbm, wv_hbm, wo_hbm, out_gain_hbm, list_hbm, count_hbm,
    out_ref,
    buf, wq, wk, wv, wo, in_gain, out_gain, lists, counts, qpad, kbuf, vtbuf, peak, total, acc, mask, hn, hn_in,
    load_sem, send_sem, recv_sem, pass_send, pass_recv, misc_send, misc_recv,
):
    chips = views // 2
    me = lax.axis_index("views")
    chip, core = me // 2, me % 2
    sign = 1 - 2 * core
    place = ring_position(chip, chips)
    partner = chip * 2 + 1 - core
    half = wq.shape[1]
    rows = tok_hbm.shape[0]
    heads = half // HEAD_DIM
    route, arrive, settle = ring_route(chips)

    def device(step):
        return {"views": ring_chip(place + step * sign, chips) * 2 + core}

    columns = pl.ds(pl.multiple_of(core * half, half), half)
    loads = [
        pltpu.make_async_copy(tok_hbm, buf.at[0, 0], load_sem.at[0]),
        pltpu.make_async_copy(wq_hbm.at[:, columns], wq, load_sem.at[1]),
        pltpu.make_async_copy(wk_hbm.at[:, columns], wk, load_sem.at[2]),
        pltpu.make_async_copy(wv_hbm.at[:, columns], wv, load_sem.at[3]),
        pltpu.make_async_copy(wo_hbm, wo, load_sem.at[4]),
        pltpu.make_async_copy(in_gain_hbm, in_gain, load_sem.at[5]),
        pltpu.make_async_copy(out_gain_hbm, out_gain, load_sem.at[6]),
        pltpu.make_async_copy(list_hbm, lists.at[0], load_sem.at[7]),
        pltpu.make_async_copy(count_hbm, counts.at[0], load_sem.at[8]),
    ]

    barrier = pltpu.get_barrier_semaphore()
    for way in (-1, 1):
        pl.semaphore_signal(barrier, inc=1, device_id=device(way), device_id_type=MESH)
    pl.semaphore_signal(barrier, inc=1, device_id={"views": partner}, device_id_type=MESH)
    for load in loads:
        load.start()
    pl.semaphore_wait(barrier, 3)

    size = rows // PARTS

    def hop(slot, part):
        source, step = route[slot]
        span = pl.ds(part * size, size)
        return pltpu.make_async_remote_copy(
            src_ref=tok_hbm.at[span] if source == 0 else buf.at[source, 0, span],
            dst_ref=buf.at[slot, 0, span],
            send_sem=send_sem.at[slot, part],
            recv_sem=recv_sem.at[slot, part],
            device_id=device(step),
            device_id_type=MESH,
        )

    def hand_over(slot, part):
        span = pl.ds(part * size, size)
        return pltpu.make_async_remote_copy(
            src_ref=tok_hbm.at[span] if slot == 0 else buf.at[slot, 0, span],
            dst_ref=buf.at[slot, 1, span],
            send_sem=pass_send.at[slot, part],
            recv_sem=pass_recv.at[slot, part],
            device_id={"views": partner},
            device_id_type=MESH,
        )

    list_copy = pltpu.make_async_remote_copy(
        src_ref=list_hbm, dst_ref=lists.at[1], send_sem=misc_send.at[0], recv_sem=misc_recv.at[0],
        device_id={"views": partner}, device_id_type=MESH,
    )
    count_copy = pltpu.make_async_remote_copy(
        src_ref=count_hbm, dst_ref=counts.at[1], send_sem=misc_send.at[2], recv_sem=misc_recv.at[2],
        device_id={"views": partner}, device_id_type=MESH,
    )
    swap = pltpu.make_async_remote_copy(
        src_ref=hn.at[1], dst_ref=hn_in, send_sem=misc_send.at[1], recv_sem=misc_recv.at[1],
        device_id={"views": partner}, device_id_type=MESH,
    )
    parts = range(PARTS)
    list_copy.start()
    count_copy.start()
    for part in parts:
        hand_over(0, part).start()
        for slot in route:
            if route[slot][0] == 0:
                hop(slot, part).start()

    peak[...] = jnp.full(peak.shape, -INF, jnp.float32)
    total[...] = jnp.zeros(total.shape, jnp.float32)
    acc[...] = jnp.zeros(acc.shape, jnp.float32)
    for load in loads[5:]:
        load.wait()
    list_copy.wait_recv()
    count_copy.wait_recv()
    ids = jnp.zeros((16, 1), jnp.int32)
    line = lax.broadcasted_iota(jnp.int32, (16, 1), 0)
    for t in range(CHUNKS):
        for bank in range(2):
            way = sign * (1 - 2 * bank)
            slot = slot_of(jnp.int32(t), place, way, chips)
            odd = slot % 2
            step = (slot + 1) // 2 * (2 * odd - 1) * way
            view = ring_chip(place + step, chips) * 2 + (core if bank == 0 else 1 - core)
            ids = jnp.where(line == 2 * t + bank, view, ids)
    for side, query_view in enumerate((me, partner)):
        listed = lists[side]
        valid = lax.broadcasted_iota(jnp.int32, (16, listed.shape[1]), 1) < counts[side:side + 1, :]
        hits = jnp.where(((listed == ids) | (ids == query_view)) & valid, 1.0, 0.0)
        mask[:, side * rows:(side + 1) * rows] = jnp.broadcast_to(
            jnp.max(hits, axis=1, keepdims=True), (16, rows)
        )

    def normed_of(first, second):
        raw = jnp.concatenate([buf[first, 0], buf[second, 1]], axis=0).astype(jnp.float32)
        mean_sq = jnp.mean(raw * raw, axis=-1, keepdims=True)
        return (raw * lax.rsqrt(mean_sq + 1e-6) * in_gain[...]).astype(jnp.bfloat16)

    loads[0].wait()
    for part in parts:
        hand_over(0, part).wait_recv()
    loads[1].wait()
    query = jnp.dot(normed_of(0, 0), wq[...], preferred_element_type=jnp.float32).astype(jnp.bfloat16)
    query = query.astype(jnp.float32) * HEAD_DIM ** (-0.5)
    query_t = query.T.astype(jnp.bfloat16)
    zero = jnp.zeros((HEAD_DIM, 2 * rows), jnp.bfloat16)
    for h in range(heads):
        mine = query_t[h * HEAD_DIM:(h + 1) * HEAD_DIM, :]
        qpad[h] = jnp.concatenate([mine, zero] if h % 2 == 0 else [zero, mine], axis=0)
    loads[2].wait()
    loads[3].wait()

    def chunk(slot, carry):
        for ahead_of, handed in settle.items():
            @pl.when(slot == ahead_of)
            def _(handed=handed):
                for got, part in handed:
                    hand_over(got, part).wait_recv()

        near = slot_of(slot, place, sign, chips)
        far = slot_of(slot, place, -sign, chips)
        normed = normed_of(near, far)
        kbuf[...] = jnp.dot(normed, wk[...], preferred_element_type=jnp.float32).astype(jnp.bfloat16)
        value = jnp.dot(normed, wv[...], preferred_element_type=jnp.float32)
        vtbuf[...] = value.T.astype(jnp.bfloat16)
        on_first = mask[pl.ds(2 * slot, 1), :] > 0.5
        on_second = mask[pl.ds(2 * slot + 1, 1), :] > 0.5
        def scores_of(h):
            pair = (h // 2) * 2 * HEAD_DIM
            return jnp.dot(kbuf[:, pair:pair + 2 * HEAD_DIM], qpad[h], preferred_element_type=jnp.float32)

        waiting = scores_of(0)
        pend = None
        def finish(p):
            h, keep, weights = p
            feats = slice(h * HEAD_DIM, (h + 1) * HEAD_DIM)
            acc[feats, :] = acc[feats, :] * keep + jnp.dot(vtbuf[feats, :], weights, preferred_element_type=jnp.float32)
        peaks, totals = peak[...], total[...]
        new_peaks, new_totals = [], []
        for h in range(heads):
            scores = waiting
            if h + 1 < heads:
                waiting = scores_of(h + 1)
            first, second = scores[:rows], scores[rows:]
            old = peaks[h:h + 1, :]
            new = jnp.maximum(
                jnp.where(on_first, jnp.max(first, axis=0, keepdims=True), -INF),
                jnp.where(on_second, jnp.max(second, axis=0, keepdims=True), -INF),
            )
            new = jnp.maximum(old, new)
            e_first = jnp.exp(first - jnp.where(on_first, new, INF))
            e_second = jnp.exp(second - jnp.where(on_second, new, INF))
            keep = jnp.exp(old - new)
            new_peaks.append(new)
            new_totals.append(totals[h:h + 1, :] * keep + jnp.sum(e_first + e_second, axis=0, keepdims=True))
            weights = jnp.concatenate([e_first.astype(jnp.bfloat16), e_second.astype(jnp.bfloat16)], axis=0)
            if pend is not None:
                finish(pend)
            pend = (h, keep, weights)
        finish(pend)
        peak[...] = jnp.concatenate(new_peaks, axis=0)
        total[...] = jnp.concatenate(new_totals, axis=0)

        for after, arrivals in arrive.items():
            @pl.when(slot == after)
            def _(arrivals=arrivals):
                for got, part in arrivals:
                    hop(got, part).wait_recv()
                    for later in route:
                        if route[later][0] == got:
                            hop(later, part).start()
                    hand_over(got, part).start()
        return carry

    lax.fori_loop(0, CHUNKS, chunk, 0)

    gain = out_gain[:, columns]
    pieces = []
    for h in range(heads):
        attended = acc[h * HEAD_DIM:(h + 1) * HEAD_DIM, :] / total[h:h + 1, :]
        mean_sq = jnp.mean(attended * attended, axis=0, keepdims=True)
        pieces.append(attended * lax.rsqrt(mean_sq + 1e-6))
    head_normed = (jnp.concatenate(pieces, axis=0).T * gain).astype(jnp.bfloat16)
    hn[1] = head_normed[rows:]
    swap.start()
    hn[0] = head_normed[:rows]
    loads[4].wait()
    others = pl.ds(pl.multiple_of((1 - core) * half, half), half)
    update = jnp.dot(hn[0], wo[columns, :], preferred_element_type=jnp.float32)
    swap.wait_recv()
    update = update + jnp.dot(hn_in[...], wo[others, :], preferred_element_type=jnp.float32)
    out_ref[...] = (buf[0, 0].astype(jnp.float32) + update).astype(out_ref.dtype)

    for part in parts:
        for slot in route:
            hop(slot, part).wait_send()
        for slot in range(len(route) + 1):
            hand_over(slot, part).wait_send()
    list_copy.wait_send()
    count_copy.wait_send()
    swap.wait_send()


def on_device(tokens, in_gain, w_query, w_key, w_value, w_out, out_gain, covis_list, covis_count):
    views = lax.axis_size("views")
    rows, width = tokens.shape[1:]
    half = width // 2
    slots = len(ring_route(views // 2)[0]) + 1
    slots_listed = covis_list.shape[1]
    hbm = pl.BlockSpec(memory_space=pltpu.HBM)
    vmem = pl.BlockSpec(memory_space=pltpu.VMEM)
    bf16, f32 = jnp.bfloat16, jnp.float32
    heads = half // HEAD_DIM
    dma = pltpu.SemaphoreType.DMA
    out = pl.pallas_call(
        functools.partial(body, views),
        out_shape=jax.ShapeDtypeStruct((rows, width), tokens.dtype),
        in_specs=[hbm] * 9,
        out_specs=vmem,
        scratch_shapes=[
            pltpu.VMEM((slots, 2, rows, width), bf16),
            pltpu.VMEM((width, half), bf16),
            pltpu.VMEM((width, half), bf16),
            pltpu.VMEM((width, half), bf16),
            pltpu.VMEM((width, width), bf16),
            pltpu.VMEM((1, width), f32),
            pltpu.VMEM((1, width), f32),
            pltpu.VMEM((2, 1, slots_listed), jnp.int32),
            pltpu.VMEM((2, 1), jnp.int32),
            pltpu.VMEM((heads, 2 * HEAD_DIM, 2 * rows), bf16),
            pltpu.VMEM((2 * rows, half), bf16),
            pltpu.VMEM((half, 2 * rows), bf16),
            pltpu.VMEM((heads, 2 * rows), f32),
            pltpu.VMEM((heads, 2 * rows), f32),
            pltpu.VMEM((half, 2 * rows), f32),
            pltpu.VMEM((16, 2 * rows), f32),
            pltpu.VMEM((2, rows, half), bf16),
            pltpu.VMEM((rows, half), bf16),
            dma((9,)),
            dma((slots, PARTS)),
            dma((slots, PARTS)),
            dma((slots, PARTS)),
            dma((slots, PARTS)),
            dma((3,)),
            dma((3,)),
        ],
        compiler_params=pltpu.CompilerParams(
            collective_id=0, has_side_effects=True, vmem_limit_bytes=60 * 1024 * 1024
        ),
    )(tokens[0], in_gain[None], w_query, w_key, w_value, w_out, out_gain[None], covis_list, covis_count)
    return out[None]


def solution(mesh):
    in_specs = (
        P(("groups", "views"), None, None),
        P(), P(), P(), P(), P(), P(),
        P(("groups", "views"), None),
        P(("groups", "views")),
    )
    out_specs = P(("groups", "views"), None, None)
    return jax.shard_map(on_device, mesh=mesh, in_specs=in_specs, out_specs=out_specs, check_vma=False)
```
